32 devices in a mesh: tile: 4 (over x, core), frame: 8 (over z, y).
Axes of the slice: x: 2, y: 2, z: 4, core: 2. Of those that a mesh axis runs over, the one named last changes fastest.
Arguments:
- queries: bfloat16 [8192, 1536], P(('tile', 'frame')), may hold values from -5 to 5
- keys: bfloat16 [8192, 1536], P(('tile', 'frame')), may hold values from -5 to 5
- values: bfloat16 [8192, 1536], P(('tile', 'frame')), may hold values from -6 to 6
- block_lists: int32 [64, 26], replicated, may hold values from -1 to 63, as said below
Outputs:
- attended: bfloat16 [8192, 1536], P(('tile', 'frame'))
The draws below stay inside these ranges and needn't reach their ends.
Inputs may be any that keep to these rules, and one draw needn't show every extreme that they name: `block_lists`: block b belongs to spatial tile (b // 2) // 8 and frame group (b // 2) % 8. Row b lists first, without repeats, the key blocks that query block b attends to, then -1 to its end. Every listed block lies at a squared distance of at most 4 from block b in (tile, frame group), and all blocks of b's own tile and frame group are listed.
All inputs are finite; a program needn't handle non-finite values.
Results may differ from the reference program's by a relative error of at most 0.004.
Values may be sent and summed in bfloat16 or wider, within the bound.
A program may use at most 128 MiB of HBM per device.

```python
import math
import jax
import jax.numpy as jnp
from jax import lax

HEADS = 12
DH = 128
BLK = 128
BLK_DEV = 2
WIDTH = 1536
TILES = 4
GROUPS = 8
TOKENS = 8192
QBLOCKS = 64
LIST = 26


def offset_pairs():
    return [(across, along) for across in range(-2, 3) for along in range(-2, 3) if across * across + along * along <= 4]


def draw_block_lists(key, part):
    pairs = offset_pairs()
    tile_off = jnp.array([entry[0] for entry in pairs], jnp.int32)
    group_off = jnp.array([entry[1] for entry in pairs], jnp.int32)
    reach_sq = tile_off * tile_off + group_off * group_off
    blocks = jnp.arange(QBLOCKS, dtype=jnp.int32)
    device = blocks // BLK_DEV
    tile_of = device // GROUPS
    group_of = device % GROUPS
    radius = jax.random.randint(key, (QBLOCKS,), 1, 4)
    centre = (TILES // 2 * GROUPS + GROUPS // 2) * BLK_DEV
    radius = jnp.where(blocks == centre, 3, radius)
    limit_sq = jnp.where(radius == 3, 4, radius)
    tile_key = tile_of[:, None] + tile_off[None, :]
    group_key = group_of[:, None] + group_off[None, :]
    usable = (reach_sq[None, :] <= limit_sq[:, None]) & (tile_key >= 0) & (tile_key < TILES) & (group_key >= 0) & (group_key < GROUPS)
    base_block = (tile_key * GROUPS + group_key) * BLK_DEV
    within = jnp.arange(BLK_DEV, dtype=jnp.int32)
    block_ids = (base_block[:, :, None] + within[None, None, :]).reshape(QBLOCKS, LIST)
    usable = jnp.broadcast_to(usable[:, :, None], (QBLOCKS, len(pairs), BLK_DEV)).reshape(QBLOCKS, LIST)
    ordering_key = jnp.where(usable, 0, LIST) + jnp.arange(LIST, dtype=jnp.int32)[None, :]
    permuted = jnp.argsort(ordering_key, axis=1)
    block_ids = jnp.take_along_axis(block_ids, permuted, axis=1)
    usable = jnp.take_along_axis(usable, permuted, axis=1)
    return jnp.where(usable, block_ids, -1).astype(jnp.int32)


def base_field(key, scale, salt):
    noise_key = jax.random.fold_in(key, salt)
    field = jax.random.normal(noise_key, (TOKENS, WIDTH), jnp.float32) * scale
    return jnp.clip(field, -5.0, 5.0)


def draw_queries(key, part):
    field = base_field(key, 1.3, 1)
    return field.astype(jnp.bfloat16)


def draw_keys(key, part):
    field = base_field(key, 1.3, 2)
    return field.astype(jnp.bfloat16)


def draw_values(key, part):
    offsets = jax.random.normal(jax.random.fold_in(key, 4), (QBLOCKS, WIDTH), jnp.float32)
    noise = jax.random.normal(jax.random.fold_in(key, 3), (TOKENS, WIDTH), jnp.float32)
    field = noise + jnp.repeat(offsets, BLK, axis=0)
    return jnp.clip(field, -6.0, 6.0).astype(jnp.bfloat16)


def setup_inputs(seed: int = 0) -> dict:
    streams_of = jax.random.split(jax.random.key(seed), 5)
    queries = draw_queries(jax.random.fold_in(streams_of[4], 71), 0)
    keys = draw_keys(jax.random.fold_in(streams_of[4], 71), 0)
    values = draw_values(jax.random.fold_in(streams_of[4], 71), 0)
    block_lists = draw_block_lists(jax.random.fold_in(streams_of[4], 71), 0)
    return dict(queries=queries, keys=keys, values=values, block_lists=block_lists)


def reference(queries, keys, values, block_lists):
    query_blocks = queries.reshape(QBLOCKS, BLK, HEADS, DH)
    key_blocks = keys.reshape(QBLOCKS, BLK, HEADS, DH)
    value_blocks = values.reshape(QBLOCKS, BLK, HEADS, DH)
    scale = 1.0 / math.sqrt(DH)

    def one_block(inputs):
        query_rows, listed = inputs
        listed_ok = listed >= 0
        picked = jnp.where(listed_ok, listed, 0).astype(jnp.int32)
        key_rows = key_blocks[picked].reshape(LIST * BLK, HEADS, DH)
        value_rows = value_blocks[picked].reshape(LIST * BLK, HEADS, DH)
        allowed = jnp.repeat(listed_ok, BLK)
        scores = jnp.einsum('qhd,khd->hqk', query_rows.astype(jnp.float32), key_rows.astype(jnp.float32)) * scale
        masked = jnp.where(allowed[None, None, :], scores, -1e+30)
        top = lax.optimization_barrier(jnp.max(masked, axis=2, keepdims=True))
        weights = jnp.where(allowed[None, None, :], jnp.exp(masked - top), 0.0)
        denom = lax.optimization_barrier(jnp.sum(weights, axis=2))
        rounded = lax.optimization_barrier(weights.astype(jnp.bfloat16)).astype(jnp.float32)
        mixed = jnp.einsum('hqk,khd->qhd', rounded, value_rows.astype(jnp.float32))
        result = mixed / denom.T[:, :, None]
        return result.reshape(BLK, HEADS * DH).astype(jnp.bfloat16)
    outputs = lax.map(one_block, (query_blocks, block_lists))
    return outputs.reshape(QBLOCKS * BLK, HEADS * DH)
```

```python
import functools
import math

import jax
import jax.numpy as jnp
from jax import lax
from jax.experimental import pallas as pl
from jax.experimental.pallas import tpu as pltpu
from jax.sharding import PartitionSpec as P

HEADS = 12
DH = 128
BLK = 128
CHUNKS = 3
PER = HEADS // CHUNKS
HALF = PER * DH
NEGATIVE = -1e30
SCALE = math.log2(math.e) / math.sqrt(DH)

SELF, PART, NEAR, ZA, ZB, X1, X2, X3, DIAG, PNEAR, PDIAG, XNEAR, XDIAG = range(13)
SLOTS = 13
GROUPS_OF_SLOTS = (
    (SELF,),
    (PART,),
    (NEAR, ZA, ZB, X1, X2, X3),
    (DIAG, PNEAR, XNEAR),
    (PDIAG, XDIAG),
)


def geometry():
    tiles, groups = lax.axis_size("tile"), lax.axis_size("frame")
    t, g = lax.axis_index("tile"), lax.axis_index("frame")
    f = 2 * lax.rem(t, 2) - 1
    d = 2 * lax.rem(g, 2) - 1
    offsets = (
        (0, 0), (-f, 0), (0, -d), (0, 2 * d), (0, -2 * d), (f, 0), (2 * f, 0), (-2 * f, 0),
        (0, d), (-f, -d), (-f, d), (f, -d), (f, d),
    )
    return tiles, groups, t, g, f, d, offsets


def kernel(q_ref, k_ref, v_ref, bias_ref, o_ref, buf, acc, top, total, own_sem, send_sem, recv_sem):
    tiles, groups, t, g, f, d, offsets = geometry()

    def inside(dt, dg):
        a, b = t + dt, g + dg
        return (a >= 0) & (a < tiles) & (b >= 0) & (b < groups)

    valid = [inside(*offset) for offset in offsets]
    peers = ((-f, 0), (0, -d), (0, 2), (0, -2), (f, 0), (2, 0), (-2, 0))

    def own_copy(j, which):
        ref = (k_ref, v_ref)[which]
        return pltpu.make_async_copy(
            ref.at[:, pl.ds(j * HALF, HALF)],
            buf.at[SELF, j, :, pl.ds(which * HALF, HALF)],
            own_sem.at[j, which],
        )

    for j in range(CHUNKS):
        for which in range(2):
            own_copy(j, which).start()

    barrier = pltpu.get_barrier_semaphore()
    for dt, dg in peers:
        @pl.when(inside(dt, dg))
        def _():
            pl.semaphore_signal(
                barrier, inc=1, device_id=(t + dt, g + dg), device_id_type=pl.DeviceIdType.MESH
            )
    pl.semaphore_wait(barrier, sum(inside(*peer).astype(jnp.int32) for peer in peers))

    every = (0, 1, 2)
    moves = (
        (SELF, NEAR, (0, -d), True, every),
        (SELF, ZA, (0, -2 * d), True, every),
        (SELF, ZB, (0, 2 * d), True, every),
        (SELF, X1, (f, 0), True, every),
        (SELF, X2, (-2 * f, 0), True, every),
        (SELF, PART, (-f, 0), True, every),
        (NEAR, DIAG, (0, -2 * d), True, (0, 1)),
        (ZB, DIAG, (0, -d), True, (2,)),
        (NEAR, XNEAR, (f, 0), True, (2,)),
        (X1, XNEAR, (0, -d), True, (0, 1)),
        (NEAR, PNEAR, (-f, 0), True, every),
        (X1, X3, (-f, 0), True, every),
        (DIAG, XDIAG, (f, 0), True, every),
        (DIAG, PDIAG, (-f, 0), True, every),
    )

    def among(j, chunks):
        hit = j == chunks[0]
        for other in chunks[1:]:
            hit = hit | (j == other)
        return hit

    def each_move(j, sources, act):
        for index, (source, slot, place, _, chunks) in enumerate(moves):
            if source not in sources:
                continue
            where = inside(*place) & valid[source]
            if len(chunks) < CHUNKS:
                where = where & among(j, chunks)

            @pl.when(where)
            def _():
                act(
                    pltpu.make_async_remote_copy(
                        src_ref=buf.at[source, j],
                        dst_ref=buf.at[slot, j],
                        send_sem=send_sem.at[index, j],
                        recv_sem=recv_sem.at[slot, j],
                        device_id=(t + place[0], g + place[1]),
                        device_id_type=pl.DeviceIdType.MESH,
                    )
                )

    def arrived(slot, j):
        pltpu.make_async_copy(buf.at[slot, j], buf.at[slot, j], recv_sem.at[slot, j]).wait()

    lane = lax.broadcasted_iota(jnp.int32, (1, 2 * BLK), 1)

    def compute(slot, j):
        upper = jnp.where(lane < BLK, bias_ref[4 * slot], bias_ref[4 * slot + 1])
        lower = jnp.where(lane < BLK, bias_ref[4 * slot + 2], bias_ref[4 * slot + 3])
        for hh in range(PER):
            head = j * PER + hh
            cols = pl.ds(pl.multiple_of(head * DH, DH), DH)
            k = buf[slot, j, :, hh * DH:(hh + 1) * DH]
            v = buf[slot, j, :, HALF + hh * DH:HALF + (hh + 1) * DH]
            s = lax.dot_general(
                q_ref[:, cols], k, (((1,), (1,)), ((), ())), preferred_element_type=jnp.float32
            )
            s = jnp.concatenate([s[:BLK] * SCALE + upper, s[BLK:] * SCALE + lower], axis=0)
            peak = jnp.max(s, axis=1, keepdims=True)
            if slot == SELF:
                new = jnp.broadcast_to(peak, (2 * BLK, DH))
            else:
                old = top[head]
                new = jnp.maximum(old, peak)
            p = jnp.exp2(s - jnp.concatenate([new, new], axis=1))
            part = p[:, :DH] + p[:, DH:]
            mixed = jnp.dot(p.astype(jnp.bfloat16), v, preferred_element_type=jnp.float32)
            if slot != SELF:
                rescale = jnp.exp2(old - new)
                part = part + total[head] * rescale
                mixed = mixed + acc[:, cols] * rescale
            top[head] = new
            total[head] = part
            acc[:, cols] = mixed

    for j in range(CHUNKS):
        own_copy(j, 0).wait()
        own_copy(j, 1).wait()
        each_move(j, (SELF,), lambda copy: copy.start())

    for members in GROUPS_OF_SLOTS:
        def step(j, carry):
            if members != (SELF,):
                for slot in members:
                    @pl.when(valid[slot])
                    def _():
                        arrived(slot, j)
                    each_move(j, (slot,), lambda copy: copy.start())
            for slot in members:
                @pl.when(valid[slot])
                def _():
                    compute(slot, j)
            return carry
        lax.fori_loop(0, CHUNKS, step, 0)

    for head in range(HEADS):
        denom = jnp.sum(total[head], axis=1, keepdims=True)
        cols = slice(head * DH, (head + 1) * DH)
        o_ref[:, cols] = (acc[:, cols] / denom).astype(jnp.bfloat16)

    def drain(j, carry):
        each_move(j, tuple(range(SLOTS)), lambda copy: copy.wait_send())
        return carry
    lax.fori_loop(0, CHUNKS, drain, 0)


def shards(queries, keys, values, block_lists):
    tiles, groups, t, g, f, d, offsets = geometry()
    rows, width = queries.shape
    nblocks = rows // BLK
    start = (t * groups + g) * nblocks
    own = lax.dynamic_slice(block_lists, (start, jnp.int32(0)), (nblocks, block_lists.shape[1]))
    first = jnp.stack([((t + dt) * groups + g + dg) * nblocks for dt, dg in offsets])
    ids = first[:, None, None] + jnp.arange(nblocks, dtype=jnp.int32)[None, None, :]
    hit = jnp.any(own[None, :, None, :] == ids[..., None], axis=3)
    bias = jnp.where(hit, 0.0, NEGATIVE).astype(jnp.float32).reshape(-1)
    vmem = pl.BlockSpec(memory_space=pltpu.VMEM)
    return pl.pallas_call(
        kernel,
        out_shape=jax.ShapeDtypeStruct((rows, width), jnp.bfloat16),
        in_specs=[
            vmem,
            pl.BlockSpec(memory_space=pl.ANY),
            pl.BlockSpec(memory_space=pl.ANY),
            pl.BlockSpec(memory_space=pltpu.SMEM),
        ],
        out_specs=vmem,
        scratch_shapes=[
            pltpu.VMEM((SLOTS, CHUNKS, rows, 2 * HALF), jnp.bfloat16),
            pltpu.VMEM((rows, width), jnp.float32),
            pltpu.VMEM((HEADS, rows, DH), jnp.float32),
            pltpu.VMEM((HEADS, rows, DH), jnp.float32),
            pltpu.SemaphoreType.DMA((CHUNKS, 2)),
            pltpu.SemaphoreType.DMA((14, CHUNKS)),
            pltpu.SemaphoreType.DMA((SLOTS, CHUNKS)),
        ],
        compiler_params=pltpu.CompilerParams(
            collective_id=0, has_side_effects=True, vmem_limit_bytes=48 * 1024 * 1024
        ),
    )(queries, keys, values, bias)


def solution(mesh):
    placed = P(("tile", "frame"), None)
    return jax.shard_map(
        shards, mesh=mesh, in_specs=(placed, placed, placed, P()), out_specs=placed, check_vma=False
    )
```

```python
import functools
import math

import jax
import jax.numpy as jnp
from jax import lax
from jax.experimental import pallas as pl
from jax.experimental.pallas import tpu as pltpu
from jax.sharding import PartitionSpec as P

HEADS = 12
DH = 128
BLK = 128
CHUNKS = 3
PER = HEADS // CHUNKS
HALF = PER * DH
NEGATIVE = -1e30
SCALE = math.log2(math.e) / math.sqrt(DH)

SELF, PART, NEAR, ZA, ZB, X1, X2, X3, DIAG, PNEAR, PDIAG, XNEAR, XDIAG = range(13)
SLOTS = 13
STAGES = (
    (0, (SELF,)),
    (1, (PART, NEAR, ZA, ZB, X1, X2)),
    (2, (DIAG, X3, PNEAR, XNEAR)),
    (3, (PDIAG, XDIAG)),
)
RELAYED = (NEAR, ZB, X1, DIAG)
DIAG_Z, DIAG_Y = (0,), (1, 2)
XNEAR_X, XNEAR_Y = (0, 1), (2,)


def geometry():
    tiles, groups = lax.axis_size("tile"), lax.axis_size("frame")
    t, g = lax.axis_index("tile"), lax.axis_index("frame")
    f = 2 * lax.rem(t, 2) - 1
    d = 2 * lax.rem(g, 2) - 1
    offsets = (
        (0, 0), (-f, 0), (0, -d), (0, 2 * d), (0, -2 * d), (f, 0), (2 * f, 0), (-2 * f, 0),
        (0, d), (-f, -d), (-f, d), (f, -d), (f, d),
    )
    return tiles, groups, t, g, f, d, offsets


def kernel(q_hbm, k_ref, v_ref, lists_ref, o_ref, q_ref, bias, buf, acc, top, total, q_sem, own_sem, send_sem, recv_sem):
    tiles, groups, t, g, f, d, offsets = geometry()

    def inside(dt, dg):
        a, b = t + dt, g + dg
        return (a >= 0) & (a < tiles) & (b >= 0) & (b < groups)

    valid = [inside(*offset) for offset in offsets]
    peers = ((-f, 0), (0, -d), (0, 2), (0, -2), (f, 0), (2, 0), (-2, 0))

    def own_copy(j, which):
        ref = (k_ref, v_ref)[which]
        return pltpu.make_async_copy(
            ref.at[:, pl.ds(j * HALF, HALF)],
            buf.at[SELF, j, :, pl.ds(which * HALF, HALF)],
            own_sem.at[j, which],
        )

    for j in range(CHUNKS):
        for which in range(2):
            own_copy(j, which).start()
    q_copy = pltpu.make_async_copy(q_hbm, q_ref, q_sem)
    q_copy.start()

    barrier = pltpu.get_barrier_semaphore()
    for dt, dg in peers:
        @pl.when(inside(dt, dg))
        def _():
            pl.semaphore_signal(
                barrier, inc=1, device_id=(t + dt, g + dg), device_id_type=pl.DeviceIdType.MESH
            )
    pl.semaphore_wait(barrier, sum(inside(*peer).astype(jnp.int32) for peer in peers))

    every = tuple(range(CHUNKS))
    moves = (
        (SELF, NEAR, (0, -d), every),
        (SELF, ZA, (0, -2 * d), every),
        (SELF, ZB, (0, 2 * d), every),
        (SELF, X1, (f, 0), every),
        (SELF, X2, (-2 * f, 0), every),
        (SELF, PART, (-f, 0), every),
        (NEAR, DIAG, (0, -2 * d), DIAG_Z),
        (ZB, DIAG, (0, -d), DIAG_Y),
        (NEAR, XNEAR, (f, 0), XNEAR_X),
        (X1, XNEAR, (0, -d), XNEAR_Y),
        (NEAR, PNEAR, (-f, 0), every),
        (X1, X3, (-f, 0), every),
        (DIAG, XDIAG, (f, 0), every),
        (DIAG, PDIAG, (-f, 0), every),
    )

    def among(j, chunks):
        hit = j == chunks[0]
        for other in chunks[1:]:
            hit = hit | (j == other)
        return hit

    def each_move(j, sources, act):
        for index, (source, slot, place, chunks) in enumerate(moves):
            if source not in sources:
                continue
            where = inside(*place) & valid[source]
            if len(chunks) < CHUNKS:
                where = where & among(j, chunks)

            @pl.when(where)
            def _():
                act(
                    pltpu.make_async_remote_copy(
                        src_ref=buf.at[source, j],
                        dst_ref=buf.at[slot, j],
                        send_sem=send_sem.at[index, j],
                        recv_sem=recv_sem.at[slot, j],
                        device_id=(t + place[0], g + place[1]),
                        device_id_type=pl.DeviceIdType.MESH,
                    )
                )

    def arrived(slot, j):
        pltpu.make_async_copy(buf.at[slot, j], buf.at[slot, j], recv_sem.at[slot, j]).wait()

    def finish(j):
        for hh in range(PER):
            head = j * PER + hh
            cols = pl.ds(pl.multiple_of(head * DH, DH), DH)
            denom = jnp.sum(total[head], axis=1, keepdims=True)
            o_ref[:, cols] = (acc[:, cols] / denom).astype(jnp.bfloat16)

    def mask_rows():
        lists = lists_ref[...]
        block = lax.broadcasted_iota(jnp.int32, lists.shape, 1)
        second = lax.broadcasted_iota(jnp.int32, (1, 2 * BLK), 1) // BLK
        for half in range(2):
            mine = 2 * (t * groups + g) + half
            listed = jnp.sum(jnp.where(block == mine, lists, 0), axis=1, keepdims=True)
            for slot, (dt, dg) in enumerate(offsets):
                ids = 2 * ((t + dt) * groups + g + dg) + second
                hit = jnp.max(jnp.where(listed == ids, 1, 0), axis=0, keepdims=True)
                bias[2 * slot + half:2 * slot + half + 1, :] = jnp.where(hit > 0, 0.0, NEGATIVE)

    def compute(slot, j):
        upper = bias[2 * slot:2 * slot + 1, :]
        lower = bias[2 * slot + 1:2 * slot + 2, :]
        for hh in range(PER):
            head = j * PER + hh
            cols = pl.ds(pl.multiple_of(head * DH, DH), DH)
            k = buf[slot, j, :, hh * DH:(hh + 1) * DH]
            v = buf[slot, j, :, HALF + hh * DH:HALF + (hh + 1) * DH]
            s = lax.dot_general(
                q_ref[:, cols], k, (((1,), (1,)), ((), ())), preferred_element_type=jnp.float32
            )
            s = jnp.concatenate([s[:BLK] * SCALE + upper, s[BLK:] * SCALE + lower], axis=0)
            peak = jnp.max(s, axis=1, keepdims=True)
            if slot == SELF:
                new = jnp.broadcast_to(peak, (2 * BLK, DH))
            else:
                old = top[head]
                new = jnp.maximum(old, peak)
            p = jnp.exp2(s - jnp.concatenate([new, new], axis=1))
            part = p[:, :DH] + p[:, DH:]
            mixed = jnp.dot(p.astype(jnp.bfloat16), v, preferred_element_type=jnp.float32)
            if slot != SELF:
                rescale = jnp.exp2(old - new)
                part = part + total[head] * rescale
                mixed = mixed + acc[:, cols] * rescale
            top[head] = new
            total[head] = part
            acc[:, cols] = mixed

    def step(tick, carry):
        @pl.when(tick < CHUNKS)
        def _():
            own_copy(tick, 0).wait()
            own_copy(tick, 1).wait()
            each_move(tick, (SELF,), lambda copy: copy.start())

        @pl.when(tick == 0)
        def _():
            mask_rows()
            q_copy.wait()

        for lag, members in STAGES:
            j = tick - lag

            @pl.when((j >= 0) & (j < CHUNKS))
            def _():
                for slot in members:
                    if slot in RELAYED:
                        @pl.when(valid[slot])
                        def _():
                            arrived(slot, j)
                        each_move(j, (slot,), lambda copy: copy.start())
        for lag, members in STAGES:
            j = tick - lag

            @pl.when((j >= 0) & (j < CHUNKS))
            def _():
                for slot in members:
                    @pl.when(valid[slot])
                    def _():
                        if slot != SELF and slot not in RELAYED:
                            arrived(slot, j)
                        compute(slot, j)
                if members == STAGES[-1][1]:
                    finish(j)
        return carry
    lax.fori_loop(0, CHUNKS + STAGES[-1][0], step, 0)

    def drain(j, carry):
        each_move(j, tuple(range(SLOTS)), lambda copy: copy.wait_send())
        return carry
    lax.fori_loop(0, CHUNKS, drain, 0)


def shards(queries, keys, values, block_lists):
    rows, width = queries.shape
    vmem = pl.BlockSpec(memory_space=pltpu.VMEM)
    return pl.pallas_call(
        kernel,
        out_shape=jax.ShapeDtypeStruct((rows, width), jnp.bfloat16),
        in_specs=[
            pl.BlockSpec(memory_space=pl.ANY),
            pl.BlockSpec(memory_space=pl.ANY),
            pl.BlockSpec(memory_space=pl.ANY),
            vmem,
        ],
        out_specs=vmem,
        scratch_shapes=[
            pltpu.VMEM((rows, width), jnp.bfloat16),
            pltpu.VMEM((2 * SLOTS, rows), jnp.float32),
            pltpu.VMEM((SLOTS, CHUNKS, rows, 2 * HALF), jnp.bfloat16),
            pltpu.VMEM((rows, width), jnp.float32),
            pltpu.VMEM((HEADS, rows, DH), jnp.float32),
            pltpu.VMEM((HEADS, rows, DH), jnp.float32),
            pltpu.SemaphoreType.DMA,
            pltpu.SemaphoreType.DMA((CHUNKS, 2)),
            pltpu.SemaphoreType.DMA((14, CHUNKS)),
            pltpu.SemaphoreType.DMA((SLOTS, CHUNKS)),
        ],
        compiler_params=pltpu.CompilerParams(
            collective_id=0, has_side_effects=True, vmem_limit_bytes=67043328
        ),
    )(queries, keys, values, block_lists.T)


def solution(mesh):
    placed = P(("tile", "frame"), None)
    return jax.shard_map(
        shards, mesh=mesh, in_specs=(placed, placed, placed, P()), out_specs=placed, check_vma=False
    )
```
